32 devices in a mesh: work: 8 (over z, y), firm: 4 (over x, core).
Axes of the slice: x: 2, y: 2, z: 4, core: 2. Of those that a mesh axis runs over, the one named last changes fastest.
Arguments:
- worker_feat: bfloat16 [64, 16384], P('firm', 'work'), may hold values from -4 to 4
- firm_feat: bfloat16 [64, 16384], P('work', 'firm'), may hold values from -1.75 to 1.75
- worker_pot: float32 [16384], P('work'), may hold values from -1 to 1
- firm_pot: float32 [16384], P('firm'), may hold values from -1 to 1
- worker_caps: int32 [16384], P('work'), may hold values from 1 to 5
- firm_caps: int32 [16384], P('firm'), may hold values from 1 to 5
Outputs:
- step_workers: float32 [16384], P('work')
- step_firms: float32 [16384], P('firm')
The draws below stay inside these ranges and needn't reach their ends.
All inputs are finite; a program needn't handle non-finite values.
Results may differ from the reference program's by a relative error of at most 0.0003.
Values may be sent and summed in bfloat16 or wider, within the bound.
A program may use at most 64 MiB of HBM per device.

```python
import math
import jax
import jax.numpy as jnp
from jax import lax

R = 64
ITERS = 4
I = 16384
J = 16384


def firm_values(key):
    folded = jax.random.fold_in(key, 7101)
    magnitude = jax.random.uniform(jax.random.fold_in(folded, 1), (R, J), jnp.float32, 0.5, 1.5)
    polarity = jax.random.bernoulli(jax.random.fold_in(folded, 2), 0.5, (R, J))
    return jnp.where(polarity, magnitude, -magnitude)


def draw_firm_feat(key, part):
    return firm_values(key).astype(jnp.bfloat16)


def draw_worker_feat(key, part):
    firm_all = firm_values(key)
    folded = jax.random.fold_in(key, 7202)
    background = jax.random.truncated_normal(jax.random.fold_in(folded, 1), -4.0, 4.0, (R, I), jnp.float32)
    partner = jax.random.randint(jax.random.fold_in(folded, 2), (I,), 0, J)
    planted = jax.random.bernoulli(jax.random.fold_in(folded, 3), 1.0 / 256.0, (I,))
    target = math.log(J) + math.log(10.0)
    factor = target / math.sqrt(R)
    partner_cols = firm_all[:, partner]
    aligned = jnp.where(partner_cols >= 0.0, factor, -factor)
    return jnp.where(planted[None, :], aligned, background).astype(jnp.bfloat16)


def set_ends(array, stream_key, low, top_value):
    longest = array.shape.index(max(array.shape))
    spots = []
    for shift in (0, 1):
        where = [jax.random.randint(jax.random.fold_in(stream_key, axis), (), 0, length) for axis, length in enumerate(array.shape)]
        where[longest] = (where[longest] + shift) % array.shape[longest]
        spots.append(tuple(where))
    return array.at[spots[0]].set(low).at[spots[1]].set(top_value)


def shard_levels(key, extent, split, smallest, high):
    level, own = 1.0, jax.random.fold_in(key, 6)
    for dim, shards_of in split:
        draws = jnp.exp(jax.random.uniform(jax.random.fold_in(own, dim), (shards_of,), jnp.float32, smallest / len(split), high / len(split)))
        level = level * jnp.repeat(draws, extent[dim] // shards_of).reshape([-1 if axis == dim else 1 for axis in range(len(extent))])
    return level


def setup_inputs(seed: int = 0) -> dict:
    key_of = jax.random.split(jax.random.key(seed), 7)
    return {
        "worker_feat": draw_worker_feat(jax.random.fold_in(key_of[6], 71), 0),
        "firm_feat": draw_firm_feat(jax.random.fold_in(key_of[6], 71), 0),
        "worker_pot": jnp.clip(jax.random.uniform(key_of[2], (I,), jnp.float32, -1.0, 1.0) * shard_levels(key_of[2], (I,), ((0, 8),), -0.4, 0.0), -1.0, 1.0),
        "firm_pot": jnp.clip(jax.random.uniform(key_of[3], (J,), jnp.float32, -1.0, 1.0) * shard_levels(key_of[3], (J,), ((0, 4),), -0.4, 0.0), -1.0, 1.0),
        "worker_caps": set_ends(jax.random.randint(key_of[4], (I,), 1, 6), jax.random.fold_in(key_of[4], 1), 1, 5).astype(jnp.int32),
        "firm_caps": set_ends(jax.random.randint(key_of[5], (J,), 1, 2 + 4 * I // J), jax.random.fold_in(key_of[5], 1), 1, (2 + 4 * I // J) - 1).astype(jnp.int32),
    }


def kernel_pass(worker_feat, firm_feat, worker_pot, firm_pot, vec_u, vec_v):
    total_rows = worker_feat.shape[1]
    total_cols = firm_feat.shape[1]
    block = math.gcd(total_rows, 512)
    count = total_rows // block
    scale = 1.0 / math.sqrt(R)
    inverse = 1.0 / J

    def step(cols_acc, index):
        start = (index * block).astype(jnp.int32)
        feat_blk = lax.dynamic_slice_in_dim(worker_feat, start, block, 1)
        pot_blk = lax.dynamic_slice_in_dim(worker_pot, start, block, 0)
        vec_blk = lax.dynamic_slice_in_dim(vec_u, start, block, 0)
        surplus = lax.dot_general(feat_blk, firm_feat, (((0,), (0,)), ((), ())), preferred_element_type=jnp.float32)
        kernel = jnp.exp(surplus * scale - pot_blk[:, None] - firm_pot[None, :]) * inverse
        rows = jnp.dot(kernel, vec_v, precision=lax.Precision.HIGHEST)
        cols_acc = cols_acc + jnp.dot(vec_blk, kernel, precision=lax.Precision.HIGHEST)
        return (cols_acc, rows)
    cols, rows = lax.scan(step, jnp.zeros((total_cols,), jnp.float32), jnp.arange(count, dtype=jnp.int32))
    return (rows.reshape(total_rows), cols)

def reference(worker_feat, firm_feat, worker_pot, firm_pot, worker_caps, firm_caps):
    ones_u = jnp.ones(worker_pot.shape, jnp.float32)
    ones_v = jnp.ones(firm_pot.shape, jnp.float32)
    row_total, col_total = kernel_pass(worker_feat, firm_feat, worker_pot, firm_pot, ones_u, ones_v)
    diag_u = row_total + jnp.exp(-worker_pot)
    diag_v = col_total + jnp.exp(-firm_pot)
    rhs_u = diag_u - worker_caps.astype(jnp.float32)
    rhs_v = diag_v - firm_caps.astype(jnp.float32)
    step_u = jnp.zeros_like(rhs_u)
    step_v = jnp.zeros_like(rhs_v)
    res_u, res_v = (rhs_u, rhs_v)
    dir_u, dir_v = (rhs_u, rhs_v)
    norm_now = jnp.sum(res_u * res_u) + jnp.sum(res_v * res_v)
    for index in range(ITERS):
        prod_u, prod_v = kernel_pass(worker_feat, firm_feat, worker_pot, firm_pot, dir_u, dir_v)
        image_u = diag_u * dir_u + prod_u
        image_v = diag_v * dir_v + prod_v
        alpha = norm_now / (jnp.sum(dir_u * image_u) + jnp.sum(dir_v * image_v))
        step_u = step_u + alpha * dir_u
        step_v = step_v + alpha * dir_v
        res_u = res_u - alpha * image_u
        res_v = res_v - alpha * image_v
        norm_next = jnp.sum(res_u * res_u) + jnp.sum(res_v * res_v)
        dir_u = res_u + norm_next / norm_now * dir_u
        dir_v = res_v + norm_next / norm_now * dir_v
        norm_now = norm_next
    return (step_u, step_v)
```

```python
import functools
import math

import jax
import jax.numpy as jnp
from jax import lax
from jax.experimental import pallas as pl
from jax.experimental.pallas import tpu as pltpu
from jax.sharding import PartitionSpec as P

ITERS = 4
CHUNK = 256
KEEP_BYTES = 40 << 20
MESH = pl.DeviceIdType.MESH


def fold(x):
    total = x[:, 0:128]
    for k in range(1, x.shape[1] // 128):
        total = total + x[:, 128 * k:128 * (k + 1)]
    return total


def kernel(nf, nw, kept, wf_ref, ff_ref, wp_ref, fp_ref, wc_ref, fc_ref, su_ref, sv_ref,
           e_ref, ub, racc, cacc, vb, wt, ft, wslots, fslots, wide_w, wide_f, rows_ref,
           rslots, cslots, sslots, f_send, f_recv, w_send, w_recv, s_send, s_recv):
    R = wf_ref.shape[1]
    C = ff_ref.shape[1]
    feats = wt.shape[1]
    chunks = R // CHUNK
    scale = 1.0 / math.sqrt(feats)
    inverse = 1.0 / (C * nf)
    fi = lax.axis_index("firm")
    wi = lax.axis_index("work")
    W = min(1024, C)
    parts = W // 128

    barrier = pltpu.get_barrier_semaphore()
    for d in range(1, nf):
        pl.semaphore_signal(barrier, 1, device_id={"firm": lax.rem(fi + d, nf)}, device_id_type=MESH)
    for d in range(1, nw):
        pl.semaphore_signal(barrier, 1, device_id={"work": lax.rem(wi + d, nw)}, device_id_type=MESH)
    pl.semaphore_wait(barrier, nf + nw - 2)

    def send_firm(src, dst, stage):
        copies = []
        for d in range(1, nf):
            copy = pltpu.make_async_remote_copy(
                src_ref=src, dst_ref=dst, send_sem=f_send.at[stage, d], recv_sem=f_recv.at[stage, d],
                device_id={"firm": lax.rem(fi + d, nf)}, device_id_type=MESH)
            copy.start()
            copies.append(copy)
        return copies

    def send_work(src, dst, send, recv, stage):
        copies = []
        for d in range(1, nw):
            copy = pltpu.make_async_remote_copy(
                src_ref=src, dst_ref=dst, send_sem=send.at[stage, d], recv_sem=recv.at[stage, d],
                device_id={"work": lax.rem(wi + d, nw)}, device_id_type=MESH)
            copy.start()
            copies.append(copy)
        return copies

    def finish(copies):
        for copy in copies:
            copy.wait()

    g_work = send_work(ff_ref, fslots.at[wi], w_send, w_recv, 0)
    g_firm = send_firm(wf_ref, wslots.at[fi], 0)
    wslots[fi] = wf_ref[...]
    fslots[wi] = ff_ref[...]
    exp_w = jnp.exp(-wp_ref[...])
    exp_f = jnp.exp(-fp_ref[...])
    left = exp_w
    right = exp_f * inverse

    def set_ub(x):
        for k in range(R // 128):
            ub[128 * k:128 * (k + 1), :] = jnp.transpose(
                jnp.broadcast_to(x[:, 128 * k:128 * (k + 1)], (128, 128)))

    def set_vb(y):
        vb[...] = jnp.broadcast_to(y, (8, C))

    set_ub(left)
    set_vb(right)
    finish(g_firm)
    fr = wf_ref.shape[0]
    for k in range(nf):
        wide_w[fr * k:fr * (k + 1), :] = wslots[k].astype(jnp.float32)
    for k in range(R // 128):
        wt[128 * k:128 * (k + 1), :] = jnp.transpose(wide_w[:, 128 * k:128 * (k + 1)]).astype(jnp.bfloat16)
    finish(g_work)
    wr = ff_ref.shape[0]
    for k in range(nw):
        wide_f[wr * k:wr * (k + 1), :] = fslots[k].astype(jnp.float32)
    ft[...] = wide_f[...].astype(jnp.bfloat16)

    def build(row0, slot0):
        for cb in range(C // 512):
            s = jnp.dot(wt[pl.ds(row0, CHUNK), :], ft[:, 512 * cb:512 * (cb + 1)],
                        preferred_element_type=jnp.float32)
            e_ref[pl.ds(slot0, CHUNK), 512 * cb:512 * (cb + 1)] = jnp.exp(s * scale)

    def sweep(row0, slot0, with_cols):
        unroll = 4
        for cb in range(C // W):
            base = cb * W
            vecs = [vb[:, base + 128 * j:base + 128 * (j + 1)] for j in range(parts)]

            def step(g, accs):
                accs = list(accs)
                for k in range(unroll):
                    off = pl.multiple_of(g * (8 * unroll), 8 * unroll) + 8 * k
                    src = pl.multiple_of(slot0 + off, 8)
                    row = pl.multiple_of(row0 + off, 8)
                    u = ub[pl.ds(row, 8), :]
                    total = racc[pl.ds(row, 8), :]
                    for j in range(parts):
                        e = e_ref[pl.ds(src, 8), base + 128 * j:base + 128 * (j + 1)]
                        total = total + e * vecs[j]
                        if with_cols:
                            accs[j] = accs[j] + e * u
                    racc[pl.ds(row, 8), :] = total
                return tuple(accs)

            init = ()
            if with_cols:
                init = tuple(cacc[:, base + 128 * j:base + 128 * (j + 1)] for j in range(parts))
            accs = lax.fori_loop(0, CHUNK // (8 * unroll), step, init)
            if with_cols:
                for j in range(parts):
                    cacc[:, base + 128 * j:base + 128 * (j + 1)] = accs[j]

    def kernel_pass(first, with_cols):
        racc[...] = jnp.zeros_like(racc)
        if with_cols:
            cacc[...] = jnp.zeros_like(cacc)

        def held(c, _):
            row0 = pl.multiple_of(c * CHUNK, CHUNK)
            if first:
                build(row0, row0)
            sweep(row0, row0, with_cols)
            return 0

        lax.fori_loop(0, kept, held, 0)
        if kept < chunks:
            def rest(c, _):
                row0 = pl.multiple_of(c * CHUNK, CHUNK)
                build(row0, kept * CHUNK)
                sweep(row0, kept * CHUNK, with_cols)
                return 0

            lax.fori_loop(kept, chunks, rest, 0)

    def row_part():
        for k in range(R // 128):
            block = jnp.transpose(racc[128 * k:128 * (k + 1), :])
            rows_ref[:, 128 * k:128 * (k + 1)] = jnp.sum(block, axis=0, keepdims=True)
        return rows_ref[...] * left

    def col_part():
        return jnp.sum(cacc[...], axis=0, keepdims=True) * right

    def total_of(ref, stage, n, cut):
        total = ref[stage, 0, :, cut]
        for k in range(1, n):
            total = total + ref[stage, k, :, cut]
        return total

    rows_cut = slice(0, R)
    dots_cut = slice(R, R + 256)

    def send_cols(stage):
        cslots[stage, wi] = col_part()
        return send_work(cslots.at[stage, wi], cslots.at[stage, wi], w_send, w_recv, stage + 1)

    kernel_pass(True, True)
    c_copies = send_cols(0)
    rslots[0, fi, :, rows_cut] = row_part()
    r_copies = send_firm(rslots.at[0, fi, :, rows_cut], rslots.at[0, fi, :, rows_cut], 1)
    finish(r_copies)
    diag_u = total_of(rslots, 0, nf, rows_cut) + exp_w
    finish(c_copies)
    diag_v = total_of(cslots, 0, nw, slice(0, C)) + exp_f
    res_u = diag_u - wc_ref[...].astype(jnp.float32)
    res_v = diag_v - fc_ref[...].astype(jnp.float32)

    count_u = jnp.where(fi == 0, 1.0, 0.0)
    count_v = jnp.where(wi == 0, 1.0, 0.0)
    dir_u = dir_v = along_u = along_v = step_u = step_v = None
    norm_now = alpha = None
    for index in range(ITERS):
        last = index + 1 == ITERS
        stage = index + 1
        set_ub(res_u * left)
        set_vb(res_v * right)
        kernel_pass(False, not last)
        sq_u = res_u * res_u
        sq_v = res_v * res_v
        norms = fold(sq_u) * count_u + fold(sq_v) * count_v
        diags = fold(diag_u * sq_u) * count_u + fold(diag_v * sq_v) * count_v
        if not last:
            c_copies = send_cols(stage)
            part = row_part()
            rslots[stage, fi, :, rows_cut] = part
            cross = fold(part * res_u)
            sent = slice(0, R + 256)
        else:
            cross = jnp.sum(racc[...] * ub[...], axis=0, keepdims=True)
            sent = dots_cut
        rslots[stage, fi, :, slice(R, R + 128)] = norms
        rslots[stage, fi, :, slice(R + 128, R + 256)] = diags + 2.0 * cross
        r_copies = send_firm(rslots.at[stage, fi, :, sent], rslots.at[stage, fi, :, sent], stage + 1)
        finish(r_copies)
        sslots[index, wi] = total_of(rslots, stage, nf, dots_cut)
        s_copies = send_work(sslots.at[index, wi], sslots.at[index, wi], s_send, s_recv, index)
        if not last:
            image_u = diag_u * res_u + total_of(rslots, stage, nf, rows_cut)
            finish(c_copies)
            image_v = diag_v * res_v + total_of(cslots, stage, nw, slice(0, C))
        finish(s_copies)
        dots = total_of(sslots, index, nw, slice(0, 256))
        norm_next = jnp.sum(dots[:, 0:128], axis=1, keepdims=True)
        product = jnp.sum(dots[:, 128:256], axis=1, keepdims=True)
        if index == 0:
            alpha = norm_next / product
            dir_u, dir_v = res_u, res_v
            step_u, step_v = alpha * dir_u, alpha * dir_v
            along_u, along_v = image_u, image_v
        else:
            ratio = norm_next / norm_now
            alpha = norm_next / (product - ratio * norm_next / alpha)
            dir_u = res_u + ratio * dir_u
            dir_v = res_v + ratio * dir_v
            step_u = step_u + alpha * dir_u
            step_v = step_v + alpha * dir_v
            if not last:
                along_u = image_u + ratio * along_u
                along_v = image_v + ratio * along_v
        if not last:
            res_u = res_u - alpha * along_u
            res_v = res_v - alpha * along_v
        norm_now = norm_next
    su_ref[...] = step_u
    sv_ref[...] = step_v


def body(worker_feat, firm_feat, worker_pot, firm_pot, worker_caps, firm_caps):
    nf = lax.axis_size("firm")
    nw = lax.axis_size("work")
    fr, R = worker_feat.shape
    wr, C = firm_feat.shape
    feats = fr * nf
    chunks = R // CHUNK
    kept = min(chunks, KEEP_BYTES // (CHUNK * C * 4))
    held_rows = (kept if kept == chunks else kept + 1) * CHUNK
    f32 = jnp.float32
    dma = pltpu.SemaphoreType.DMA
    vmem = pl.BlockSpec(memory_space=pltpu.VMEM)
    su, sv = pl.pallas_call(
        functools.partial(kernel, nf, nw, kept),
        out_shape=(jax.ShapeDtypeStruct((1, R), f32), jax.ShapeDtypeStruct((1, C), f32)),
        in_specs=[vmem] * 6,
        out_specs=(vmem, vmem),
        scratch_shapes=[
            pltpu.VMEM((held_rows, C), f32),
            pltpu.VMEM((R, 128), f32),
            pltpu.VMEM((R, 128), f32),
            pltpu.VMEM((8, C), f32),
            pltpu.VMEM((8, C), f32),
            pltpu.VMEM((R, feats), jnp.bfloat16),
            pltpu.VMEM((feats, C), jnp.bfloat16),
            pltpu.VMEM((nf, fr, R), jnp.bfloat16),
            pltpu.VMEM((nw, wr, C), jnp.bfloat16),
            pltpu.VMEM((feats, R), f32),
            pltpu.VMEM((feats, C), f32),
            pltpu.VMEM((1, R), f32),
            pltpu.VMEM((ITERS + 1, nf, 1, R + 256), f32),
            pltpu.VMEM((ITERS, nw, 1, C), f32),
            pltpu.VMEM((ITERS, nw, 1, 256), f32),
            dma((ITERS + 2, nf)), dma((ITERS + 2, nf)),
            dma((ITERS + 1, nw)), dma((ITERS + 1, nw)),
            dma((ITERS, nw)), dma((ITERS, nw)),
        ],
        compiler_params=pltpu.CompilerParams(
            collective_id=0, has_side_effects=True, vmem_limit_bytes=60 << 20),
    )(worker_feat, firm_feat, worker_pot[None, :], firm_pot[None, :],
      worker_caps[None, :], firm_caps[None, :])
    return su.reshape(R), sv.reshape(C)


def solution(mesh):
    placed = (P("firm", "work"), P("work", "firm"), P("work"), P("firm"), P("work"), P("firm"))
    return jax.shard_map(
        body, mesh=mesh, in_specs=placed, out_specs=(P("work"), P("firm")), check_vma=False
    )
```

```python
import functools
import math

import jax
import jax.numpy as jnp
from jax import lax
from jax.experimental import pallas as pl
from jax.experimental.pallas import tpu as pltpu
from jax.sharding import PartitionSpec as P

ITERS = 4
CHUNK = 256
KEEP_BYTES = 40 << 20
MESH = pl.DeviceIdType.MESH


def fold(x):
    total = x[:, 0:128]
    for k in range(1, x.shape[1] // 128):
        total = total + x[:, 128 * k:128 * (k + 1)]
    return total


def kernel(nf, nw, kept, wf_ref, ff_ref, wp_ref, fp_ref, wc_ref, fc_ref, su_ref, sv_ref,
           e_ref, ub, racc, cacc, vb, wt, ft, wslots, fslots, wide_w, wide_f, rows_ref,
           rslots, cslots, sslots, f_send, f_recv, w_send, w_recv, s_send, s_recv, g_send, g_recv):
    R = wf_ref.shape[1]
    C = ff_ref.shape[1]
    feats = wt.shape[1]
    chunks = R // CHUNK
    scale = 1.0 / math.sqrt(feats)
    inverse = 1.0 / (C * nf)
    fi = lax.axis_index("firm")
    wi = lax.axis_index("work")
    W = min(1024, C)
    parts = W // 128

    barrier = pltpu.get_barrier_semaphore()
    for d in range(1, nf):
        pl.semaphore_signal(barrier, 1, device_id={"firm": lax.rem(fi + d, nf)}, device_id_type=MESH)
    for d in range(1, nw):
        pl.semaphore_signal(barrier, 1, device_id={"work": lax.rem(wi + d, nw)}, device_id_type=MESH)
    pl.semaphore_wait(barrier, nf + nw - 2)

    def send_firm(src, dst, stage):
        copies = []
        for d in range(1, nf):
            copy = pltpu.make_async_remote_copy(
                src_ref=src, dst_ref=dst, send_sem=f_send.at[stage, d], recv_sem=f_recv.at[stage, d],
                device_id={"firm": lax.rem(fi + d, nf)}, device_id_type=MESH)
            copy.start()
            copies.append(copy)
        return copies

    def send_work(src, dst, send, recv, stage):
        copies = []
        for d in range(1, nw):
            copy = pltpu.make_async_remote_copy(
                src_ref=src, dst_ref=dst, send_sem=send.at[stage, d], recv_sem=recv.at[stage, d],
                device_id={"work": lax.rem(wi + d, nw)}, device_id_type=MESH)
            copy.start()
            copies.append(copy)
        return copies

    def finish(copies):
        for copy in copies:
            copy.wait()

    g_firm = send_firm(wf_ref, wslots.at[fi], 0)
    g_work = []

    def send_piece():
        cb = len(g_work)
        if cb < C // W:
            span = slice(W * cb, W * (cb + 1))
            g_work.append(send_work(ff_ref.at[:, span], fslots.at[wi, :, span], g_send, g_recv, cb))

    send_piece()
    wslots[fi] = wf_ref[...]
    fslots[wi] = ff_ref[...]
    exp_w = jnp.exp(-wp_ref[...])
    exp_f = jnp.exp(-fp_ref[...])
    left = exp_w
    right = exp_f * inverse

    def set_ub(x):
        for k in range(R // 128):
            ub[128 * k:128 * (k + 1), :] = jnp.transpose(
                jnp.broadcast_to(x[:, 128 * k:128 * (k + 1)], (128, 128)))

    def set_vb(y):
        vb[...] = jnp.broadcast_to(y, (8, C))

    set_ub(left)
    set_vb(right)
    finish(g_firm)
    fr = wf_ref.shape[0]
    for k in range(nf):
        wide_w[fr * k:fr * (k + 1), :] = wslots[k].astype(jnp.float32)
    for k in range(R // 128):
        wt[128 * k:128 * (k + 1), :] = jnp.transpose(wide_w[:, 128 * k:128 * (k + 1)]).astype(jnp.bfloat16)
    wr = ff_ref.shape[0]

    def arrive(cb):
        span = slice(W * cb, W * (cb + 1))
        for copy in g_work[cb]:
            copy.wait_send()
        send_piece()
        for copy in g_work[cb]:
            copy.wait_recv()
        for k in range(nw):
            wide_f[wr * k:wr * (k + 1), span] = fslots[k, :, span].astype(jnp.float32)
        ft[:, span] = wide_f[:, span].astype(jnp.bfloat16)

    def build(row0, slot0, spans):
        for cb in spans:
            s = jnp.dot(wt[pl.ds(row0, CHUNK), :], ft[:, 512 * cb:512 * (cb + 1)],
                        preferred_element_type=jnp.float32)
            e_ref[pl.ds(slot0, CHUNK), 512 * cb:512 * (cb + 1)] = jnp.exp(s * scale)

    def sweep(row0, slot0, with_cols, spans):
        unroll = CHUNK // 8
        for cb in spans:
            base = cb * W
            vecs = [vb[:, base + 128 * j:base + 128 * (j + 1)] for j in range(parts)]

            def step(g, accs):
                accs = list(accs)
                for k in range(unroll):
                    off = pl.multiple_of(g * (8 * unroll), 8 * unroll) + 8 * k
                    src = pl.multiple_of(slot0 + off, 8)
                    row = pl.multiple_of(row0 + off, 8)
                    u = ub[pl.ds(row, 8), :]
                    total = racc[pl.ds(row, 8), :]
                    for j in range(parts):
                        e = e_ref[pl.ds(src, 8), base + 128 * j:base + 128 * (j + 1)]
                        total = total + e * vecs[j]
                        if with_cols:
                            accs[j] = accs[j] + e * u
                    racc[pl.ds(row, 8), :] = total
                return tuple(accs)

            init = ()
            if with_cols:
                init = tuple(cacc[:, base + 128 * j:base + 128 * (j + 1)] for j in range(parts))
            accs = lax.fori_loop(0, CHUNK // (8 * unroll), step, init)
            if with_cols:
                for j in range(parts):
                    cacc[:, base + 128 * j:base + 128 * (j + 1)] = accs[j]

    def kernel_pass(first, with_cols):
        racc[...] = jnp.zeros_like(racc)
        if with_cols:
            cacc[...] = jnp.zeros_like(cacc)

        def both(spans, fresh):
            cuts = [k for cb in spans for k in range(cb * W // 512, (cb + 1) * W // 512)]

            def held(c, _):
                row0 = pl.multiple_of(c * CHUNK, CHUNK)
                if fresh:
                    build(row0, row0, cuts)
                sweep(row0, row0, with_cols, spans)
                return 0

            def rest(c, _):
                row0 = pl.multiple_of(c * CHUNK, CHUNK)
                build(row0, kept * CHUNK, cuts)
                sweep(row0, kept * CHUNK, with_cols, spans)
                return 0

            lax.fori_loop(0, kept, held, 0)
            if kept < chunks:
                lax.fori_loop(kept, chunks, rest, 0)

        if first:
            for cb in range(C // W):
                arrive(cb)
                both([cb], True)
        else:
            both(list(range(C // W)), False)

    def row_part():
        for k in range(R // 128):
            block = jnp.transpose(racc[128 * k:128 * (k + 1), :])
            rows_ref[:, 128 * k:128 * (k + 1)] = jnp.sum(block, axis=0, keepdims=True)
        return rows_ref[...] * left

    def col_part():
        return jnp.sum(cacc[...], axis=0, keepdims=True) * right

    def total_of(ref, stage, n, cut):
        total = ref[stage, 0, :, cut]
        for k in range(1, n):
            total = total + ref[stage, k, :, cut]
        return total

    rows_cut = slice(0, R)
    dots_cut = slice(R, R + 256)

    def send_cols(stage, part):
        cslots[stage, wi] = part
        return send_work(cslots.at[stage, wi], cslots.at[stage, wi], w_send, w_recv, stage + 1)

    kernel_pass(True, True)
    c_copies = send_cols(0, col_part())
    rslots[0, fi, :, rows_cut] = row_part()
    r_copies = send_firm(rslots.at[0, fi, :, rows_cut], rslots.at[0, fi, :, rows_cut], 1)
    finish(r_copies)
    diag_u = total_of(rslots, 0, nf, rows_cut) + exp_w
    finish(c_copies)
    diag_v = total_of(cslots, 0, nw, slice(0, C)) + exp_f
    res_u = diag_u - wc_ref[...].astype(jnp.float32)
    res_v = diag_v - fc_ref[...].astype(jnp.float32)

    count_u = jnp.where(fi == 0, 1.0, 0.0)
    count_v = jnp.where(wi == 0, 1.0, 0.0)
    set_ub(res_u * left)
    set_vb(res_v * right)
    kernel_pass(False, True)
    part_v = col_part()
    part_u = row_part()
    dir_u = dir_v = along_u = along_v = step_u = step_v = acc_u = acc_v = None
    norm_now = alpha = None
    for index in range(ITERS):
        last = index + 1 == ITERS
        stage = index + 1
        if not last:
            c_copies = send_cols(stage, part_v)
            rslots[stage, fi, :, rows_cut] = part_u
        sent = dots_cut if last else slice(0, R + 256)
        sq_u = res_u * res_u
        sq_v = res_v * res_v
        norms = fold(sq_u) * count_u + fold(sq_v) * count_v
        diags = fold(diag_u * sq_u) * count_u + fold(diag_v * sq_v) * count_v
        rslots[stage, fi, :, slice(R, R + 128)] = norms
        rslots[stage, fi, :, slice(R + 128, R + 256)] = diags + 2.0 * fold(part_u * res_u)
        r_copies = send_firm(rslots.at[stage, fi, :, sent], rslots.at[stage, fi, :, sent], stage + 1)
        finish(r_copies)
        both_dots = total_of(rslots, stage, nf, dots_cut)
        sslots[index, wi, 0:1, :] = both_dots[:, 0:128]
        sslots[index, wi, 1:2, :] = both_dots[:, 128:256]
        s_copies = send_work(sslots.at[index, wi], sslots.at[index, wi], s_send, s_recv, index)
        if not last:
            image_u = diag_u * res_u + total_of(rslots, stage, nf, rows_cut)
            set_ub(image_u * left)
            finish(c_copies)
            image_v = diag_v * res_v + total_of(cslots, stage, nw, slice(0, C))
            set_vb(image_v * right)
            kernel_pass(False, index + 2 < ITERS)
            prod_u = row_part()
            prod_v = col_part() if index + 2 < ITERS else None
        finish(s_copies)
        dots = sslots[index, 0]
        for k in range(1, nw):
            dots = dots + sslots[index, k]
        norm_next = jnp.sum(dots[0:1, :], axis=1, keepdims=True)
        product = jnp.sum(dots[1:2, :], axis=1, keepdims=True)
        if index == 0:
            alpha = norm_next / product
            dir_u, dir_v = res_u, res_v
            step_u, step_v = alpha * dir_u, alpha * dir_v
            along_u, along_v = image_u, image_v
            acc_u, acc_v = prod_u, prod_v
        else:
            ratio = norm_next / norm_now
            alpha = norm_next / (product - ratio * norm_next / alpha)
            dir_u = res_u + ratio * dir_u
            dir_v = res_v + ratio * dir_v
            step_u = step_u + alpha * dir_u
            step_v = step_v + alpha * dir_v
            if not last:
                along_u = image_u + ratio * along_u
                along_v = image_v + ratio * along_v
                acc_u = prod_u + ratio * acc_u
                if prod_v is not None:
                    acc_v = prod_v + ratio * acc_v
        if not last:
            res_u = res_u - alpha * along_u
            res_v = res_v - alpha * along_v
            part_u = part_u - alpha * acc_u
            if prod_v is not None:
                part_v = part_v - alpha * acc_v
        norm_now = norm_next
    su_ref[...] = step_u
    sv_ref[...] = step_v


def body(worker_feat, firm_feat, worker_pot, firm_pot, worker_caps, firm_caps):
    nf = lax.axis_size("firm")
    nw = lax.axis_size("work")
    fr, R = worker_feat.shape
    wr, C = firm_feat.shape
    feats = fr * nf
    chunks = R // CHUNK
    kept = min(chunks, KEEP_BYTES // (CHUNK * C * 4))
    held_rows = (kept if kept == chunks else kept + 1) * CHUNK
    pieces = C // min(1024, C)
    f32 = jnp.float32
    dma = pltpu.SemaphoreType.DMA
    vmem = pl.BlockSpec(memory_space=pltpu.VMEM)
    su, sv = pl.pallas_call(
        functools.partial(kernel, nf, nw, kept),
        out_shape=(jax.ShapeDtypeStruct((1, R), f32), jax.ShapeDtypeStruct((1, C), f32)),
        in_specs=[vmem] * 6,
        out_specs=(vmem, vmem),
        scratch_shapes=[
            pltpu.VMEM((held_rows, C), f32),
            pltpu.VMEM((R, 128), f32),
            pltpu.VMEM((R, 128), f32),
            pltpu.VMEM((8, C), f32),
            pltpu.VMEM((8, C), f32),
            pltpu.VMEM((R, feats), jnp.bfloat16),
            pltpu.VMEM((feats, C), jnp.bfloat16),
            pltpu.VMEM((nf, fr, R), jnp.bfloat16),
            pltpu.VMEM((nw, wr, C), jnp.bfloat16),
            pltpu.VMEM((feats, R), f32),
            pltpu.VMEM((feats, C), f32),
            pltpu.VMEM((1, R), f32),
            pltpu.VMEM((ITERS + 1, nf, 1, R + 256), f32),
            pltpu.VMEM((ITERS, nw, 1, C), f32),
            pltpu.VMEM((ITERS, nw, 2, 128), f32),
            dma((ITERS + 2, nf)), dma((ITERS + 2, nf)),
            dma((ITERS + 1, nw)), dma((ITERS + 1, nw)),
            dma((ITERS, nw)), dma((ITERS, nw)),
            dma((pieces, nw)), dma((pieces, nw)),
        ],
        compiler_params=pltpu.CompilerParams(
            collective_id=0, has_side_effects=True, vmem_limit_bytes=60 << 20),
    )(worker_feat, firm_feat, worker_pot[None, :], firm_pot[None, :],
      worker_caps[None, :], firm_caps[None, :])
    return su.reshape(R), sv.reshape(C)


def solution(mesh):
    placed = (P("firm", "work"), P("work", "firm"), P("work"), P("firm"), P("work"), P("firm"))
    return jax.shard_map(
        body, mesh=mesh, in_specs=placed, out_specs=(P("work"), P("firm")), check_vma=False
    )
```

```python
import functools
import math

import jax
import jax.numpy as jnp
from jax import lax
from jax.experimental import pallas as pl
from jax.experimental.pallas import tpu as pltpu
from jax.sharding import PartitionSpec as P

ITERS = 4
CHUNK = 256
KEEP_BYTES = 40 << 20
MESH = pl.DeviceIdType.MESH


def fold(x):
    total = x[:, 0:128]
    for k in range(1, x.shape[1] // 128):
        total = total + x[:, 128 * k:128 * (k + 1)]
    return total


def kernel(nf, nw, kept, wf_ref, ff_ref, wp_ref, fp_ref, wc_ref, fc_ref, su_ref, sv_ref,
           e_ref, ub, racc, cacc, vb, wt, ft, wslots, fslots, wide_w, wide_f, rows_ref,
           rslots, cslots, sslots, f_send, f_recv, w_send, w_recv, s_send, s_recv, g_send, g_recv):
    R = wf_ref.shape[1]
    C = ff_ref.shape[1]
    feats = wt.shape[1]
    chunks = R // CHUNK
    scale = 1.0 / math.sqrt(feats)
    inverse = 1.0 / (C * nf)
    fi = lax.axis_index("firm")
    wi = lax.axis_index("work")
    W = min(1024, C)
    parts = W // 128

    barrier = pltpu.get_barrier_semaphore()
    for d in range(1, nf):
        pl.semaphore_signal(barrier, 1, device_id={"firm": lax.rem(fi + d, nf)}, device_id_type=MESH)
    for d in range(1, nw):
        pl.semaphore_signal(barrier, 1, device_id={"work": lax.rem(wi + d, nw)}, device_id_type=MESH)
    pl.semaphore_wait(barrier, nf + nw - 2)

    def send_firm(src, dst, stage):
        copies = []
        for d in range(1, nf):
            copy = pltpu.make_async_remote_copy(
                src_ref=src, dst_ref=dst, send_sem=f_send.at[stage, d], recv_sem=f_recv.at[stage, d],
                device_id={"firm": lax.rem(fi + d, nf)}, device_id_type=MESH)
            copy.start()
            copies.append(copy)
        return copies

    def send_work(src, dst, send, recv, stage):
        copies = []
        for d in range(1, nw):
            copy = pltpu.make_async_remote_copy(
                src_ref=src, dst_ref=dst, send_sem=send.at[stage, d], recv_sem=recv.at[stage, d],
                device_id={"work": lax.rem(wi + d, nw)}, device_id_type=MESH)
            copy.start()
            copies.append(copy)
        return copies

    def finish(copies):
        for copy in copies:
            copy.wait()

    g_firm = send_firm(wf_ref, wslots.at[fi], 0)
    g_work = []

    def send_piece():
        cb = len(g_work)
        if cb < C // W:
            span = slice(W * cb, W * (cb + 1))
            g_work.append(send_work(ff_ref.at[:, span], fslots.at[wi, :, span], g_send, g_recv, cb))

    send_piece()
    wslots[fi] = wf_ref[...]
    fslots[wi] = ff_ref[...]
    exp_w = jnp.exp(-wp_ref[...])
    exp_f = jnp.exp(-fp_ref[...])
    left = exp_w
    right = exp_f * inverse

    def set_ub(x):
        for k in range(R // 128):
            ub[128 * k:128 * (k + 1), :] = jnp.transpose(
                jnp.broadcast_to(x[:, 128 * k:128 * (k + 1)], (128, 128)))

    def set_vb(y):
        vb[...] = jnp.broadcast_to(y, (8, C))

    set_ub(left)
    set_vb(right)
    finish(g_firm)
    fr = wf_ref.shape[0]
    for k in range(nf):
        wide_w[fr * k:fr * (k + 1), :] = wslots[k].astype(jnp.float32)
    for k in range(R // 128):
        wt[128 * k:128 * (k + 1), :] = jnp.transpose(wide_w[:, 128 * k:128 * (k + 1)]).astype(jnp.bfloat16)
    wr = ff_ref.shape[0]

    def arrive(cb):
        span = slice(W * cb, W * (cb + 1))
        for copy in g_work[cb]:
            copy.wait_send()
        send_piece()
        for copy in g_work[cb]:
            copy.wait_recv()
        for k in range(nw):
            wide_f[wr * k:wr * (k + 1), span] = fslots[k, :, span].astype(jnp.float32)
        ft[:, span] = wide_f[:, span].astype(jnp.bfloat16)

    def build(row0, slot0, spans):
        for cb in spans:
            s = jnp.dot(wt[pl.ds(row0, CHUNK), :], ft[:, 512 * cb:512 * (cb + 1)],
                        preferred_element_type=jnp.float32)
            e_ref[pl.ds(slot0, CHUNK), 512 * cb:512 * (cb + 1)] = jnp.exp2(s * (scale * math.log2(math.e)))

    def sweep(row0, slot0, with_cols, spans):
        unroll = CHUNK // 8
        for cb in spans:
            base = cb * W
            vecs = [vb[:, base + 128 * j:base + 128 * (j + 1)] for j in range(parts)]

            def step(g, accs):
                accs = list(accs)
                for k in range(unroll):
                    off = pl.multiple_of(g * (8 * unroll), 8 * unroll) + 8 * k
                    src = pl.multiple_of(slot0 + off, 8)
                    row = pl.multiple_of(row0 + off, 8)
                    u = ub[pl.ds(row, 8), :]
                    total = racc[pl.ds(row, 8), :]
                    for j in range(parts):
                        e = e_ref[pl.ds(src, 8), base + 128 * j:base + 128 * (j + 1)]
                        total = total + e * vecs[j]
                        if with_cols:
                            accs[j] = accs[j] + e * u
                    racc[pl.ds(row, 8), :] = total
                return tuple(accs)

            init = ()
            if with_cols:
                init = tuple(cacc[:, base + 128 * j:base + 128 * (j + 1)] for j in range(parts))
            accs = lax.fori_loop(0, CHUNK // (8 * unroll), step, init)
            if with_cols:
                for j in range(parts):
                    cacc[:, base + 128 * j:base + 128 * (j + 1)] = accs[j]

    blocks = C // W
    ends = [blocks // 2, blocks] if blocks > 1 else [blocks]

    def kernel_pass(first, cols_stage):
        with_cols = cols_stage is not None
        copies = []
        racc[...] = jnp.zeros_like(racc)
        if with_cols:
            cacc[...] = jnp.zeros_like(cacc)

        def both(spans, fresh):
            cuts = [k for cb in spans for k in range(cb * W // 512, (cb + 1) * W // 512)]

            def held(c, _):
                row0 = pl.multiple_of(c * CHUNK, CHUNK)
                if fresh:
                    build(row0, row0, cuts)
                sweep(row0, row0, with_cols, spans)
                return 0

            def rest(c, _):
                row0 = pl.multiple_of(c * CHUNK, CHUNK)
                build(row0, kept * CHUNK, cuts)
                sweep(row0, kept * CHUNK, with_cols, spans)
                return 0

            lax.fori_loop(0, kept, held, 0)
            if kept < chunks:
                lax.fori_loop(kept, chunks, rest, 0)

        begin = 0
        for part, end in enumerate(ends):
            if first:
                for cb in range(begin, end):
                    arrive(cb)
                    both([cb], True)
            else:
                both(list(range(begin, end)), False)
            if with_cols:
                span = slice(begin * W, end * W)
                cslots[cols_stage, wi, :, span] = (
                    jnp.sum(cacc[:, span], axis=0, keepdims=True) * right[:, span])
                mine = cslots.at[cols_stage, wi, :, span]
                copies += send_work(mine, mine, w_send, w_recv, 2 * cols_stage + part)
            begin = end
        return copies

    def row_part():
        for k in range(R // 128):
            block = jnp.transpose(racc[128 * k:128 * (k + 1), :])
            rows_ref[:, 128 * k:128 * (k + 1)] = jnp.sum(block, axis=0, keepdims=True)
        return rows_ref[...] * left

    def total_of(ref, stage, n, cut):
        total = ref[stage, 0, :, cut]
        for k in range(1, n):
            total = total + ref[stage, k, :, cut]
        return total

    rows_cut = slice(0, R)
    dots_cut = slice(R, R + 256)

    c_copies = kernel_pass(True, 0)
    rslots[0, fi, :, rows_cut] = row_part()
    r_copies = send_firm(rslots.at[0, fi, :, rows_cut], rslots.at[0, fi, :, rows_cut], 1)
    finish(r_copies)
    diag_u = total_of(rslots, 0, nf, rows_cut) + exp_w
    finish(c_copies)
    diag_v = total_of(cslots, 0, nw, slice(0, C)) + exp_f
    res_u = diag_u - wc_ref[...].astype(jnp.float32)
    res_v = diag_v - fc_ref[...].astype(jnp.float32)

    count_u = jnp.where(fi == 0, 1.0, 0.0)
    count_v = jnp.where(wi == 0, 1.0, 0.0)
    set_ub(res_u * left)
    set_vb(res_v * right)
    c_copies = kernel_pass(False, 1)
    part_u = row_part()
    dir_u = dir_v = along_u = along_v = step_u = step_v = acc_u = acc_v = full_v = ratio = None
    norm_now = alpha = None
    for index in range(ITERS):
        last = index + 1 == ITERS
        stage = index + 1
        if not last:
            rslots[stage, fi, :, rows_cut] = part_u
        sent = dots_cut if last else slice(0, R + 256)
        sq_u = res_u * res_u
        sq_v = res_v * res_v
        norms = fold(sq_u) * count_u + fold(sq_v) * count_v
        diags = fold(diag_u * sq_u) * count_u + fold(diag_v * sq_v) * count_v
        rslots[stage, fi, :, slice(R, R + 128)] = norms
        rslots[stage, fi, :, slice(R + 128, R + 256)] = diags + 2.0 * fold(part_u * res_u)
        r_copies = send_firm(rslots.at[stage, fi, :, sent], rslots.at[stage, fi, :, sent], stage + 1)
        finish(r_copies)
        both_dots = total_of(rslots, stage, nf, dots_cut)
        sslots[index, wi, 0:1, :] = both_dots[:, 0:128]
        sslots[index, wi, 1:2, :] = both_dots[:, 128:256]
        s_copies = send_work(sslots.at[index, wi], sslots.at[index, wi], s_send, s_recv, index)
        if not last:
            image_u = diag_u * res_u + total_of(rslots, stage, nf, rows_cut)
            set_ub(image_u * left)
            finish(c_copies)
            got = total_of(cslots, stage, nw, slice(0, C))
            if index == 0:
                full_v = got
            else:
                acc_v = got if index == 1 else got + ratio * acc_v
                full_v = full_v - alpha * acc_v
            image_v = diag_v * res_v + full_v
            set_vb(image_v * right)
            c_copies = kernel_pass(False, index + 2 if index + 2 < ITERS else None)
            prod_u = row_part()
        finish(s_copies)
        dots = sslots[index, 0]
        for k in range(1, nw):
            dots = dots + sslots[index, k]
        norm_next = jnp.sum(dots[0:1, :], axis=1, keepdims=True)
        product = jnp.sum(dots[1:2, :], axis=1, keepdims=True)
        if index == 0:
            alpha = norm_next / product
            dir_u, dir_v = res_u, res_v
            step_u, step_v = alpha * dir_u, alpha * dir_v
            along_u, along_v = image_u, image_v
            acc_u = prod_u
        else:
            ratio = norm_next / norm_now
            alpha = norm_next / (product - ratio * norm_next / alpha)
            dir_u = res_u + ratio * dir_u
            dir_v = res_v + ratio * dir_v
            step_u = step_u + alpha * dir_u
            step_v = step_v + alpha * dir_v
            if not last:
                along_u = image_u + ratio * along_u
                along_v = image_v + ratio * along_v
                acc_u = prod_u + ratio * acc_u
        if not last:
            res_u = res_u - alpha * along_u
            res_v = res_v - alpha * along_v
            part_u = part_u - alpha * acc_u
        norm_now = norm_next
    su_ref[...] = step_u
    sv_ref[...] = step_v


def body(worker_feat, firm_feat, worker_pot, firm_pot, worker_caps, firm_caps):
    nf = lax.axis_size("firm")
    nw = lax.axis_size("work")
    fr, R = worker_feat.shape
    wr, C = firm_feat.shape
    feats = fr * nf
    chunks = R // CHUNK
    kept = min(chunks, KEEP_BYTES // (CHUNK * C * 4))
    held_rows = (kept if kept == chunks else kept + 1) * CHUNK
    pieces = C // min(1024, C)
    f32 = jnp.float32
    dma = pltpu.SemaphoreType.DMA
    vmem = pl.BlockSpec(memory_space=pltpu.VMEM)
    su, sv = pl.pallas_call(
        functools.partial(kernel, nf, nw, kept),
        out_shape=(jax.ShapeDtypeStruct((1, R), f32), jax.ShapeDtypeStruct((1, C), f32)),
        in_specs=[vmem] * 6,
        out_specs=(vmem, vmem),
        scratch_shapes=[
            pltpu.VMEM((held_rows, C), f32),
            pltpu.VMEM((R, 128), f32),
            pltpu.VMEM((R, 128), f32),
            pltpu.VMEM((8, C), f32),
            pltpu.VMEM((8, C), f32),
            pltpu.VMEM((R, feats), jnp.bfloat16),
            pltpu.VMEM((feats, C), jnp.bfloat16),
            pltpu.VMEM((nf, fr, R), jnp.bfloat16),
            pltpu.VMEM((nw, wr, C), jnp.bfloat16),
            pltpu.VMEM((feats, R), f32),
            pltpu.VMEM((feats, C), f32),
            pltpu.VMEM((1, R), f32),
            pltpu.VMEM((ITERS + 1, nf, 1, R + 256), f32),
            pltpu.VMEM((ITERS, nw, 1, C), f32),
            pltpu.VMEM((ITERS, nw, 2, 128), f32),
            dma((ITERS + 2, nf)), dma((ITERS + 2, nf)),
            dma((2 * ITERS, nw)), dma((2 * ITERS, nw)),
            dma((ITERS, nw)), dma((ITERS, nw)),
            dma((pieces, nw)), dma((pieces, nw)),
        ],
        compiler_params=pltpu.CompilerParams(
            collective_id=0, has_side_effects=True, vmem_limit_bytes=60 << 20),
    )(worker_feat, firm_feat, worker_pot[None, :], firm_pot[None, :],
      worker_caps[None, :], firm_caps[None, :])
    return su.reshape(R), sv.reshape(C)


def solution(mesh):
    placed = (P("firm", "work"), P("work", "firm"), P("work"), P("firm"), P("work"), P("firm"))
    return jax.shard_map(
        body, mesh=mesh, in_specs=placed, out_specs=(P("work"), P("firm")), check_vma=False
    )
```
